1024 devices in a mesh: gx: 16 (over x, core), gy: 64 (over y, z).
Axes of the slice: x: 8, y: 8, z: 8, core: 2. Of those that a mesh axis runs over, the one named last changes fastest.
Arguments:
- multipoles: bfloat16 [165, 262144], P(None, ('gx', 'gy')), may hold values from -6 to 6
- operators: bfloat16 [64, 165, 165], replicated, may hold values from -0.125 to 0.125
- boundary: int32 [10, 131072], P(None, ('gx', 'gy')), may hold values from 0 to 1407, as said below
- pair_target: int32 [64, 131072], P(None, ('gx', 'gy')), may hold values from 0 to 255
- pair_source: int32 [64, 131072], P(None, ('gx', 'gy')), may hold values from 0 to 1535
- pair_count: int32 [64, 1024], P(None, ('gx', 'gy')), may hold values from 1 to 128, as said below
Outputs:
- local_expansions: float32 [165, 262144], P(None, ('gx', 'gy'))
The draws below stay inside these ranges and needn't reach their ends.
Inputs may be any that keep to these rules, and one draw needn't show every extreme that they name: `boundary`: on every device and cut l, the list holds 128 distinct columns in increasing order, all below 256 + l * 128, and always includes column 256 + l * 128 - 1. `pair_count`: on every device, some class uses all 128 slots.
All inputs are finite; a program needn't handle non-finite values.
Results may differ from the reference program's by a relative error of at most 0.0003.
Values may be sent and summed in bfloat16 or wider, within the bound.
A program may use at most 64 MiB of HBM per device.

```python
import jax
import jax.numpy as jnp
from jax import lax

P_SIZE = 165
NCLASS = 64
CELLS = 256
NB = 128
W = 128
LEVELS = 10
POOL = 1536
DEVICES = 1024


def draw_boundary(key, part):
    width = CELLS + (LEVELS - 1) * NB
    scores = jax.random.randint(key, (LEVELS, DEVICES, width), 0, 1 << 18)
    column = jnp.arange(width, dtype=jnp.int32)
    column_limit = CELLS + jnp.arange(LEVELS, dtype=jnp.int32) * NB
    ranked_scores = scores * width + column[None, None, :]
    ranked_scores = jnp.where(column[None, None, :] < column_limit[:, None, None] - 1, ranked_scores, -1)
    ranked_scores = jnp.where(column[None, None, :] == column_limit[:, None, None] - 1, (1 << 18) * width + width, ranked_scores)
    _, chosen = lax.top_k(ranked_scores, NB)
    chosen = jnp.sort(chosen, axis=-1)
    return chosen.reshape(LEVELS, DEVICES * NB).astype(jnp.int32)


def draw_pair_count(key, part):
    first_key = jax.random.fold_in(key, 11)
    second_key = jax.random.fold_in(key, 12)
    counts = jax.random.randint(first_key, (NCLASS, DEVICES), 1, W + 1)
    full_class = jax.random.randint(second_key, (DEVICES,), 0, NCLASS)
    class_ids = jnp.arange(NCLASS, dtype=jnp.int32)
    counts = jnp.where(class_ids[:, None] == full_class[None, :], W, counts)
    return counts.astype(jnp.int32)


def touch_ends(entries, key, low, largest):
    place = [jax.random.randint(jax.random.fold_in(key, axis), (), 0, length) for axis, length in enumerate(entries.shape)]
    longest = entries.shape.index(max(entries.shape))
    neighbour = place[:longest] + [(place[longest] + 1) % entries.shape[longest]] + place[longest + 1:]
    return entries.at[tuple(place)].set(low).at[tuple(neighbour)].set(largest)


def levels(own_key, shape, cuts, least, largest):
    def one(position, blocks):
        draws = jax.random.uniform(jax.random.fold_in(jax.random.fold_in(own_key, 6), position), (blocks,), jnp.float32, least / len(cuts), largest / len(cuts))
        return jnp.repeat(jnp.exp(draws), shape[position] // blocks).reshape((-1,) + (1,) * (len(shape) - position - 1))

    gain = one(*cuts[0])
    for cut in cuts[1:]:
        gain = gain * one(*cut)
    return gain


def bell_draw(own_key, shape, deviation, limit, shards=(), kind=jnp.bfloat16):
    array = jax.random.normal(own_key, shape, jnp.float32) * deviation
    if len(shards) > 0:
        array = levels(own_key, shape, shards, -0.22, 0.18) * array
    return jnp.clip(array, min=-limit, max=limit).astype(kind)


def setup_inputs(seed: int = 0) -> dict:
    splits = jax.random.split(jax.random.key(seed), 7)
    return {
        "multipoles": bell_draw(splits[0], (P_SIZE, CELLS * DEVICES), 1.0, 6.0, ((1, 1024),)),
        "operators": bell_draw(splits[1], (NCLASS, P_SIZE, P_SIZE), (16 * P_SIZE) ** -0.5, 0.125),
        "boundary": draw_boundary(jax.random.fold_in(splits[6], 71), 0),
        "pair_target": touch_ends(jax.random.randint(splits[3], (NCLASS, W * DEVICES), 0, CELLS), jax.random.fold_in(splits[3], 1), 0, CELLS - 1).astype(jnp.int32),
        "pair_source": touch_ends(jax.random.randint(splits[4], (NCLASS, W * DEVICES), 0, POOL), jax.random.fold_in(splits[4], 1), 0, POOL - 1).astype(jnp.int32),
        "pair_count": draw_pair_count(jax.random.fold_in(splits[6], 71), 0),
    }


def reference(multipoles, operators, boundary, pair_target, pair_source, pair_count):
    device_ids = jnp.arange(DEVICES, dtype=jnp.int32)
    anchor = device_ids[:, None] * CELLS + jnp.arange(CELLS, dtype=jnp.int32)[None, :]
    cut_lists = boundary.reshape(LEVELS, DEVICES, NB)
    for cut_level in range(LEVELS):
        partner = device_ids ^ (1 << (LEVELS - 1 - cut_level))
        exported = jnp.take_along_axis(anchor, cut_lists[cut_level], axis=1)
        anchor = jnp.concatenate([anchor, exported[partner]], axis=1).astype(jnp.int32)
    multipole_wide = multipoles.astype(jnp.float32)
    operator_wide = operators.astype(jnp.float32)
    targets = pair_target.reshape(NCLASS, DEVICES, W).transpose(1, 0, 2)
    sources = pair_source.reshape(NCLASS, DEVICES, W).transpose(1, 0, 2)
    counts = pair_count.T
    slot_ids = jnp.arange(W, dtype=jnp.int32)

    def device_step(expansions, pieces):
        device, anchor_ids, target_rows, source_rows, device_counts = pieces
        active = slot_ids[None, :] < device_counts[:, None]
        source_ids = anchor_ids[source_rows].astype(jnp.int32)
        target_ids = (device * CELLS + target_rows).astype(jnp.int32)
        gathered = jnp.take(multipole_wide, source_ids, axis=1)
        forward_terms = jnp.einsum("cij,jcs->ics", operator_wide, gathered)
        forward_terms = jnp.where(active[None], forward_terms, 0.0)
        own_columns = jnp.take(multipole_wide, target_ids[::-1], axis=1)
        reverse_terms = jnp.einsum("cij,jcs->ics", operator_wide, own_columns)
        reverse_terms = jnp.where(active[::-1][None], reverse_terms, 0.0)
        destinations = jnp.concatenate([target_ids, source_ids[::-1]], axis=1).reshape(-1)
        all_terms = jnp.concatenate([forward_terms, reverse_terms], axis=2).reshape(P_SIZE, -1)
        return expansions.at[:, destinations].add(all_terms), None

    start = jnp.zeros((P_SIZE, DEVICES * CELLS), jnp.float32)
    expansions, _ = lax.scan(device_step, start, (device_ids, anchor, targets, sources, counts))
    return expansions
```

```python
import functools

import jax
import jax.numpy as jnp
from jax import lax
from jax.experimental import pallas as pl
from jax.experimental.pallas import tpu as pltpu
from jax.sharding import PartitionSpec as P

MESH = pl.DeviceIdType.MESH
BLOCK = 128
NT = (((1,), (1,)), ((), ()))
NN = (((1,), (0,)), ((), ()))

FLIGHT_OUT = {0: 1.5, 1: 2.5, 2: 4.0, 4: 6.0}
FLIGHT_BACK = {0: 2.0, 1: 3.5, 2: 6.0, 4: 9.0}
COST = {"terms": 9.0, "scatter": 2.4, "gather": 3.5, "out": 0.6, "back": 1.0}


def plan(distance, tiles, gathers):
    cuts = len(distance)
    order = [("R", 0), ("S", (tiles - 1, 0)), ("S", (tiles - 1, 1)), ("send", cuts - 1)]
    now = COST["terms"] + 2 * COST["scatter"]
    out, back = 0, cuts - 1
    out_due = FLIGHT_OUT[distance[0]]
    back_due = now + FLIGHT_BACK[distance[back]]
    scatters = [(tile, half) for tile in range(tiles - 2, -1, -1) for half in range(2)]
    gathers = list(range(gathers))
    while out < cuts or back >= 0 or scatters or gathers:
        if out < cuts and out_due <= now:
            order.append(("F", out))
            now += COST["out"]
            out += 1
            if out < cuts:
                out_due = now + FLIGHT_OUT[distance[out]]
            continue
        needed = bool(scatters) and back > 0 and (back + 1) // 2 <= scatters[0][0]
        if back >= 0 and back_due <= now and not needed:
            order.append(("B", back))
            now += COST["back"]
            back -= 1
            if back >= 0:
                back_due = now + FLIGHT_BACK[distance[back]]
            continue
        if scatters:
            order.append(("S", scatters.pop(0)))
            now += COST["scatter"]
        elif out == cuts and gathers:
            order.append(("G", gathers.pop(0)))
            now += COST["gather"]
        else:
            now = min([out_due] * (out < cuts) + [back_due] * (back >= 0))
    return order


def selector(index_row, first, rows):
    row = lax.broadcasted_iota(jnp.int32, (rows, index_row.shape[1]), 0) + first
    return jnp.where(row == index_row, 1.0, 0.0).astype(jnp.bfloat16)


def dot(a, b, dims=NN):
    return lax.dot_general(a, b, dims, preferred_element_type=jnp.float32)


def kernel(axes, order, multipoles, operators_hbm, boundary, pair_target, pair_source, pair_count, out,
           operators, pool, export, partial, target, source, terms, tile_sum, sums, returned, own,
           load_sem, out_send, out_recv, back_send, back_recv):
    cuts = boundary.shape[0]
    classes = pair_target.shape[0]
    coefficients = multipoles.shape[0]
    pairs = classes // 2
    low = terms.shape[1] // 2
    blocks = cuts + 2

    load = pltpu.make_async_copy(operators_hbm, operators, load_sem)
    load.start()

    def partner(cut):
        bit = cuts - 1 - cut
        inner = axes[1][1].bit_length() - 1
        name, shift = (axes[1][0], bit) if bit < inner else (axes[0][0], bit - inner)
        me = lax.axis_index(name)
        step = 1 << shift
        other = me + step - 2 * step * ((me // step) % 2)
        here = {axes[0][0]: lax.axis_index(axes[0][0]), axes[1][0]: lax.axis_index(axes[1][0])}
        here[name] = other
        return (here[axes[0][0]], here[axes[1][0]])

    barrier = pltpu.get_barrier_semaphore()
    for cut in range(cuts):
        pl.semaphore_signal(barrier, inc=1, device_id=partner(cut), device_id_type=MESH)

    def outgoing(cut):
        return pltpu.make_async_remote_copy(
            src_ref=export.at[cut], dst_ref=pool.at[cut + 2], send_sem=out_send.at[cut],
            recv_sem=out_recv.at[cut], device_id=partner(cut), device_id_type=MESH)

    def incoming(cut):
        return pltpu.make_async_remote_copy(
            src_ref=sums.at[cut + 2], dst_ref=returned.at[cut], send_sem=back_send.at[cut],
            recv_sem=back_recv.at[cut], device_id=partner(cut), device_id_type=MESH)

    def chosen(cut, first, count):
        index = boundary[pl.ds(cut, 1), :]
        total = None
        for block in range(first, first + count):
            term = dot(pool[block], selector(index, block * BLOCK, BLOCK))
            total = term if total is None else total + term
        return total

    def prepare(cut):
        if cut < cuts:
            partial[...] = chosen(cut, 0, cut + 1)

    def send_out(cut):
        if cut < cuts:
            value = partial[...] + chosen(cut, cut + 1, 1)
            export[cut] = value.astype(jnp.bfloat16)
            outgoing(cut).start()
            prepare(cut + 1)

    def split(value):
        high = value.astype(jnp.bfloat16)
        return high, (value - high.astype(jnp.float32)).astype(jnp.bfloat16)

    def add_back(cut, first, count):
        index = boundary[pl.ds(cut, 1), :]
        high, rest = split(returned[cut])
        for block in range(first, first + count):
            chooser = selector(index, block * BLOCK, BLOCK)
            sums[block] += dot(high, chooser, NT) + dot(rest, chooser, NT)

    def index_pair(ref, pair):
        return jnp.concatenate([ref[pl.ds(2 * pair, 1), :], ref[pl.ds(2 * pair + 1, 1), :]], axis=1)

    def apply(pair, value, reverse):
        results = []
        for half in range(2):
            cls = 2 * pair + half
            matrix = operators[classes - 1 - cls] if reverse else operators[cls]
            results.append(dot(matrix, value[:, half * BLOCK : (half + 1) * BLOCK]))
        return split(jnp.concatenate(results, axis=1))

    def reverse_terms():
        mine = multipoles[...]

        def one(pair):
            columns = dot(mine, selector(index_pair(target, pair), 0, mine.shape[1])).astype(jnp.bfloat16)
            high, rest = apply(pair, columns, True)
            terms[pair, 0:coefficients, :] = high
            terms[pair, low : low + coefficients, :] = rest

        def body(step, carry):
            for part in range(4):
                one(4 * step + part)
            return carry

        lax.fori_loop(0, pairs // 4, body, 0)

    def scatter(tile, part):
        tile_sum[...] = jnp.zeros_like(tile_sum)

        def body(step, carry):
            total = None
            for half in range(2):
                pair = 2 * step + half
                term = dot(terms[pair], selector(index_pair(source, pair), tile * 2 * BLOCK, 2 * BLOCK), NT)
                total = term if total is None else total + term
            tile_sum[...] += total
            return carry

        lax.fori_loop(part * pairs // 4, (part + 1) * pairs // 4, body, 0)
        total = tile_sum[0:coefficients, :] + tile_sum[low : low + coefficients, :]
        sums[2 * tile] += total[:, :BLOCK]
        sums[2 * tile + 1] += total[:, BLOCK:]

    def gather(part, parts):
        def one(pair):
            index = index_pair(source, pair)
            total = None
            for tile in range(blocks // 2):
                columns = jnp.concatenate([pool[2 * tile], pool[2 * tile + 1]], axis=1)
                term = dot(columns, selector(index, tile * 2 * BLOCK, 2 * BLOCK))
                total = term if total is None else total + term
            high, rest = apply(pair, total.astype(jnp.bfloat16), False)
            chooser = selector(index_pair(target, pair), 0, 2 * BLOCK)
            return dot(high, chooser, NT) + dot(rest, chooser, NT)

        def body(step, carry):
            own[...] += one(2 * step) + one(2 * step + 1)
            return carry

        size = pairs // parts // 2
        lax.fori_loop(part * size, (part + 1) * size, body, 0)

    pool[0] = multipoles[:, :BLOCK]
    pool[1] = multipoles[:, BLOCK:]
    slot = lax.broadcasted_iota(jnp.int32, pair_target.shape, 1)
    active = slot < pair_count[...]
    target[...] = jnp.where(active, pair_target[...], -1)
    source[...] = jnp.where(active, pair_source[...], -1)
    prepare(0)
    pl.semaphore_wait(barrier, cuts)
    send_out(0)
    sums[...] = jnp.zeros_like(sums)
    own[...] = jnp.zeros_like(own)

    gathers = sum(kind == "G" for kind, _ in order)
    for kind, number in order:
        if kind == "R":
            load.wait()
            reverse_terms()
        elif kind == "S":
            scatter(*number)
        elif kind == "G":
            gather(number, gathers)
        elif kind == "send":
            incoming(number).start()
        elif kind == "F":
            outgoing(number).wait_recv()
            send_out(number + 1)
        else:
            incoming(number).wait_recv()
            if number > 0:
                add_back(number, number + 1, 1)
                incoming(number - 1).start()
                add_back(number, 0, number + 1)
            else:
                add_back(number, 0, 2)
    out[:, :BLOCK] = sums[0] + own[:, :BLOCK]
    out[:, BLOCK:] = sums[1] + own[:, BLOCK:]
    for cut in range(cuts):
        outgoing(cut).wait_send()
        incoming(cut).wait_send()


def per_device(axes, order, multipoles, operators, boundary, pair_target, pair_source, pair_count):
    coefficients, cells = multipoles.shape
    cuts = boundary.shape[0]
    classes, slots = pair_target.shape
    vmem = pl.BlockSpec(memory_space=pltpu.VMEM)
    half_rows = -(-coefficients // 16) * 16
    return pl.pallas_call(
        functools.partial(kernel, axes, order),
        out_shape=jax.ShapeDtypeStruct((coefficients, cells), jnp.float32),
        in_specs=[vmem, pl.BlockSpec(memory_space=pl.ANY), vmem, vmem, vmem, vmem],
        out_specs=vmem,
        scratch_shapes=[
            pltpu.VMEM(operators.shape, jnp.bfloat16),
            pltpu.VMEM((cuts + 2, coefficients, BLOCK), jnp.bfloat16),
            pltpu.VMEM((cuts, coefficients, BLOCK), jnp.bfloat16),
            pltpu.VMEM((coefficients, BLOCK), jnp.float32),
            pltpu.VMEM((classes, slots), jnp.int32),
            pltpu.VMEM((classes, slots), jnp.int32),
            pltpu.VMEM((classes // 2, 2 * half_rows, 2 * slots), jnp.bfloat16),
            pltpu.VMEM((2 * half_rows, 2 * BLOCK), jnp.float32),
            pltpu.VMEM((cuts + 2, coefficients, BLOCK), jnp.float32),
            pltpu.VMEM((cuts, coefficients, BLOCK), jnp.float32),
            pltpu.VMEM((coefficients, cells), jnp.float32),
            pltpu.SemaphoreType.DMA,
            pltpu.SemaphoreType.DMA((cuts,)),
            pltpu.SemaphoreType.DMA((cuts,)),
            pltpu.SemaphoreType.DMA((cuts,)),
            pltpu.SemaphoreType.DMA((cuts,)),
        ],
        compiler_params=pltpu.CompilerParams(
            collective_id=0, has_side_effects=True, vmem_limit_bytes=60 << 20),
    )(multipoles, operators, boundary, pair_target, pair_source, pair_count)


def solution(mesh):
    axes = tuple((name, mesh.shape[name]) for name in ("gx", "gy"))
    cuts = (axes[0][1] * axes[1][1]).bit_length() - 1
    distance = [4, 2, 1, 0, 4, 2, 1, 4, 2, 1] if cuts == 10 else [1] * cuts
    order = plan(distance, (cuts + 2) // 2, 8)
    spec = P(None, ("gx", "gy"))
    return jax.shard_map(
        functools.partial(per_device, axes, order), mesh=mesh,
        in_specs=(spec, P(), spec, spec, spec, spec), out_specs=spec, check_vma=False)
```

```python
import functools

import jax
import jax.numpy as jnp
from jax import lax
from jax.experimental import pallas as pl
from jax.experimental.pallas import tpu as pltpu
from jax.sharding import PartitionSpec as P

MESH = pl.DeviceIdType.MESH
BLOCK = 128
NT = (((1,), (1,)), ((), ()))
NN = (((1,), (0,)), ((), ()))

FLIGHT_OUT = {0: 1.5, 1: 2.5, 2: 4.0, 4: 6.0}
FLIGHT_BACK = {0: 2.0, 1: 3.5, 2: 6.0, 4: 9.0}
COST = {"terms": 9.5, "scatter": 2.4, "gather": 3.5, "out": 0.6, "back": 0.8}


def plan(distance, tiles, gathers):
    cuts = len(distance)
    order = [("R", 0), ("S", (tiles - 1, 0)), ("S", (tiles - 1, 1)), ("send", cuts - 1)]
    now = COST["terms"] + 2 * COST["scatter"]
    out, back = 0, cuts - 1
    out_due = FLIGHT_OUT[distance[0]]
    back_due = now + FLIGHT_BACK[distance[back]]
    scatters = [(tile, half) for tile in range(tiles - 2, -1, -1) for half in range(2)]
    gathers = list(range(gathers))
    while out < cuts or back >= 0 or scatters or gathers:
        if out < cuts and out_due <= now:
            order.append(("F", out))
            now += COST["out"]
            out += 1
            if out < cuts:
                out_due = now + FLIGHT_OUT[distance[out]]
            continue
        needed = bool(scatters) and back > 0 and (back + 1) // 2 <= scatters[0][0]
        if back >= 0 and back_due <= now and not needed:
            order.append(("B", back))
            now += COST["back"]
            back -= 1
            if back >= 0:
                back_due = now + FLIGHT_BACK[distance[back]]
            continue
        if scatters:
            order.append(("S", scatters.pop(0)))
            now += COST["scatter"]
        elif out == cuts and gathers:
            order.append(("G", gathers.pop(0)))
            now += COST["gather"]
        else:
            now = min([out_due] * (out < cuts) + [back_due] * (back >= 0))
    return order


def selector(index_row, first, rows):
    row = lax.broadcasted_iota(jnp.int32, (rows, index_row.shape[1]), 0) + first
    return jnp.where(row == index_row, 1.0, 0.0).astype(jnp.bfloat16)


def dot(a, b, dims=NN):
    return lax.dot_general(a, b, dims, preferred_element_type=jnp.float32)


def kernel(axes, order, multipoles, operators_hbm, boundary, pair_target, pair_source, pair_count, out,
           stage, left, right, operators, pool, export, partial, target, source, terms, tile_sum, sums, returned, own,
           load_sem, out_send, out_recv, back_send, back_recv):
    cuts = boundary.shape[0]
    classes = pair_target.shape[0]
    coefficients = multipoles.shape[0]
    pairs = classes // 2
    low = terms.shape[1] // 2
    blocks = cuts + 2
    rows = sums.shape[1]
    groups, _, group, _ = stage.shape

    loads = [pltpu.make_async_copy(operators_hbm.at[:, pl.ds(g * group, group), :], stage.at[g], load_sem.at[g])
             for g in range(groups)]
    for load in reversed(loads):
        load.start()

    def partner(cut):
        bit = cuts - 1 - cut
        inner = axes[1][1].bit_length() - 1
        name, shift = (axes[1][0], bit) if bit < inner else (axes[0][0], bit - inner)
        me = lax.axis_index(name)
        step = 1 << shift
        other = me + step - 2 * step * ((me // step) % 2)
        here = {axes[0][0]: lax.axis_index(axes[0][0]), axes[1][0]: lax.axis_index(axes[1][0])}
        here[name] = other
        return (here[axes[0][0]], here[axes[1][0]])

    barrier = pltpu.get_barrier_semaphore()
    for cut in range(cuts):
        pl.semaphore_signal(barrier, inc=1, device_id=partner(cut), device_id_type=MESH)

    def outgoing(cut):
        return pltpu.make_async_remote_copy(
            src_ref=export.at[cut], dst_ref=pool.at[cut + 2], send_sem=out_send.at[cut],
            recv_sem=out_recv.at[cut], device_id=partner(cut), device_id_type=MESH)

    def incoming(cut):
        return pltpu.make_async_remote_copy(
            src_ref=sums.at[cut + 2], dst_ref=returned.at[cut, pl.ds(0, rows), :], send_sem=back_send.at[cut],
            recv_sem=back_recv.at[cut], device_id=partner(cut), device_id_type=MESH)

    def chosen(cut, first, count):
        index = boundary[pl.ds(cut, 1), :]
        total = None
        for block in range(first, first + count, 2):
            size = min(2, first + count - block)
            columns = pool[block] if size == 1 else jnp.concatenate([pool[block], pool[block + 1]], axis=1)
            term = dot(columns, selector(index, block * BLOCK, size * BLOCK))
            total = term if total is None else total + term
        return total

    def prepare(cut):
        if cut < cuts:
            partial[...] = chosen(cut, 0, cut + 1)

    def send_out(cut):
        if cut < cuts:
            value = partial[...] + chosen(cut, cut + 1, 1)
            export[cut] = value.astype(jnp.bfloat16)
            outgoing(cut).start()
            prepare(cut + 1)

    def split(value):
        high = value.astype(jnp.bfloat16)
        return jnp.concatenate([high, (value - high.astype(jnp.float32)).astype(jnp.bfloat16)], axis=0)

    def joined(value):
        return value[:rows] + value[low : low + rows]

    def add_back(cut, first, count):
        index = boundary[pl.ds(cut, 1), :]
        parts = split(returned[cut])
        for block in range(first, first + count, 2):
            size = min(2, first + count - block)
            total = joined(dot(parts, selector(index, block * BLOCK, size * BLOCK), NT))
            for part in range(size):
                sums[block + part] += total[:, part * BLOCK : (part + 1) * BLOCK]

    def index_pair(ref, pair):
        return jnp.concatenate([ref[pl.ds(2 * pair, 1), :], ref[pl.ds(2 * pair + 1, 1), :]], axis=1)

    def apply(pair, value, reverse):
        results = []
        for half in range(2):
            cls = 2 * pair + half
            matrix = operators[classes - 1 - cls] if reverse else operators[cls]
            results.append(dot(matrix, value[:, half * BLOCK : (half + 1) * BLOCK]))
        return split(jnp.concatenate(results, axis=1))

    def reverse_terms():
        mine = multipoles[...]

        def one(pair):
            columns = dot(mine, selector(index_pair(target, pair), 0, mine.shape[1])).astype(jnp.bfloat16)
            terms[pair] = apply(pair, columns, True)

        def body(step, carry):
            here = groups - 1 - step
            plain = stage[here].astype(jnp.float32).reshape(coefficients * group, coefficients)
            left[...] = plain[:, :BLOCK]
            right[:, : coefficients - BLOCK] = plain[:, BLOCK:]
            for cls in range(group):
                every = pl.ds(cls, coefficients, stride=group)
                operators[here * group + cls, 0:coefficients, :BLOCK] = left[every, :].astype(jnp.bfloat16)
                matrix = right[every, :].astype(jnp.bfloat16)
                operators[here * group + cls, 0:coefficients, BLOCK:] = matrix[:, : coefficients - BLOCK]
            for part in range(group // 2):
                one(step * (group // 2) + part)
            return carry

        lax.fori_loop(0, groups, body, 0)

    def scatter(tile, part):
        tile_sum[...] = jnp.zeros_like(tile_sum)

        def body(step, carry):
            total = None
            for half in range(2):
                pair = 2 * step + half
                term = dot(terms[pair], selector(index_pair(source, pair), tile * 2 * BLOCK, 2 * BLOCK), NT)
                total = term if total is None else total + term
            tile_sum[...] += total
            return carry

        lax.fori_loop(part * pairs // 4, (part + 1) * pairs // 4, body, 0)
        total = joined(tile_sum[...])
        sums[2 * tile] += total[:, :BLOCK]
        sums[2 * tile + 1] += total[:, BLOCK:]

    def gather(part, parts):
        def one(pair):
            index = index_pair(source, pair)
            total = None
            for tile in range(blocks // 2):
                columns = jnp.concatenate([pool[2 * tile], pool[2 * tile + 1]], axis=1)
                term = dot(columns, selector(index, tile * 2 * BLOCK, 2 * BLOCK))
                total = term if total is None else total + term
            chooser = selector(index_pair(target, pair), 0, 2 * BLOCK)
            return dot(apply(pair, total.astype(jnp.bfloat16), False), chooser, NT)

        def body(step, carry):
            own[...] += one(2 * step) + one(2 * step + 1)
            return carry

        size = pairs // parts // 2
        lax.fori_loop(part * size, (part + 1) * size, body, 0)

    pool[0] = multipoles[:, :BLOCK]
    pool[1] = multipoles[:, BLOCK:]
    slot = lax.broadcasted_iota(jnp.int32, pair_target.shape, 1)
    same = lax.broadcasted_iota(jnp.int32, (classes, classes), 0) == lax.broadcasted_iota(jnp.int32, (classes, classes), 1)
    counts = jnp.sum(jnp.where(same, pair_count[...], 0), axis=1, keepdims=True)
    active = slot < counts
    target[...] = jnp.where(active, pair_target[...], -1)
    source[...] = jnp.where(active, pair_source[...], -1)
    prepare(0)
    pl.semaphore_wait(barrier, cuts)
    send_out(0)
    sums[...] = jnp.zeros_like(sums)
    own[...] = jnp.zeros_like(own)

    gathers = sum(kind == "G" for kind, _ in order)
    for kind, number in order:
        if kind == "R":
            for load in loads:
                load.wait()
            reverse_terms()
        elif kind == "S":
            scatter(*number)
        elif kind == "G":
            gather(number, gathers)
        elif kind == "send":
            incoming(number).start()
        elif kind == "F":
            outgoing(number).wait_recv()
            send_out(number + 1)
        else:
            incoming(number).wait_recv()
            if number > 0:
                add_back(number, number + 1, 1)
                incoming(number - 1).start()
                add_back(number, 0, number + 1)
            else:
                add_back(number, 0, 2)
    for half in range(2):
        lanes = pl.ds(half * BLOCK, BLOCK)
        mine = own[0:coefficients, lanes] + own[low : low + coefficients, lanes]
        out[:, lanes] = sums[half, 0:coefficients, :] + mine
    for cut in range(cuts):
        outgoing(cut).wait_send()
        incoming(cut).wait_send()


def per_device(axes, order, multipoles, operators, boundary, pair_target, pair_source, pair_count):
    coefficients, cells = multipoles.shape
    cuts = boundary.shape[0]
    classes, slots = pair_target.shape
    vmem = pl.BlockSpec(memory_space=pltpu.VMEM)
    half_rows = -(-coefficients // 16) * 16
    rows = -(-coefficients // 8) * 8
    return pl.pallas_call(
        functools.partial(kernel, axes, order),
        out_shape=jax.ShapeDtypeStruct((coefficients, cells), jnp.float32),
        in_specs=[vmem, pl.BlockSpec(memory_space=pl.ANY), vmem, vmem, vmem, vmem],
        out_specs=vmem,
        scratch_shapes=[
            pltpu.VMEM((classes // 8, coefficients, 8, coefficients), jnp.bfloat16),
            pltpu.VMEM((coefficients * 8, BLOCK), jnp.float32),
            pltpu.VMEM((coefficients * 8, BLOCK), jnp.float32),
            pltpu.VMEM((classes, half_rows, coefficients), jnp.bfloat16),
            pltpu.VMEM((cuts + 2, coefficients, BLOCK), jnp.bfloat16),
            pltpu.VMEM((cuts, coefficients, BLOCK), jnp.bfloat16),
            pltpu.VMEM((coefficients, BLOCK), jnp.float32),
            pltpu.VMEM((classes, slots), jnp.int32),
            pltpu.VMEM((classes, slots), jnp.int32),
            pltpu.VMEM((classes // 2, 2 * half_rows, 2 * slots), jnp.bfloat16),
            pltpu.VMEM((2 * half_rows, 2 * BLOCK), jnp.float32),
            pltpu.VMEM((cuts + 2, rows, BLOCK), jnp.float32),
            pltpu.VMEM((cuts, half_rows, BLOCK), jnp.float32),
            pltpu.VMEM((2 * half_rows, cells), jnp.float32),
            pltpu.SemaphoreType.DMA((classes // 8,)),
            pltpu.SemaphoreType.DMA((cuts,)),
            pltpu.SemaphoreType.DMA((cuts,)),
            pltpu.SemaphoreType.DMA((cuts,)),
            pltpu.SemaphoreType.DMA((cuts,)),
        ],
        compiler_params=pltpu.CompilerParams(
            collective_id=0, has_side_effects=True, vmem_limit_bytes=60 << 20),
    )(multipoles, jnp.transpose(operators, (1, 0, 2)), boundary, pair_target, pair_source, pair_count.reshape(1, classes))


def solution(mesh):
    axes = tuple((name, mesh.shape[name]) for name in ("gx", "gy"))
    cuts = (axes[0][1] * axes[1][1]).bit_length() - 1
    distance = [4, 2, 1, 0, 4, 2, 1, 4, 2, 1] if cuts == 10 else [1] * cuts
    order = plan(distance, (cuts + 2) // 2, 8)
    spec = P(None, ("gx", "gy"))
    return jax.shard_map(
        functools.partial(per_device, axes, order), mesh=mesh,
        in_specs=(spec, P(), spec, spec, spec, spec), out_specs=spec, check_vma=False)
```
